32 devices in a mesh: clips: 2 (over y), tok: 4 (over z), head: 4 (over x, core).
Axes of the slice: x: 2, y: 2, z: 4, core: 2. Of those that a mesh axis runs over, the one named last changes fastest.
Arguments:
- query: bfloat16 [24, 256, 1536], P(('clips', 'tok'), 'head'), parts along dimension 0, may hold values from -16 to 16, as said below
- key: bfloat16 [24, 256, 1536], P(('clips', 'tok'), 'head'), parts along dimension 0, may hold values from -16 to 16
- value: bfloat16 [24, 256, 1536], P(('clips', 'tok'), 'head'), parts along dimension 0, may hold values from -6 to 6
- valid_rows: int32 [24], P(('clips', 'tok')), parts along dimension 0, may hold values from 1 to 8, as said below
Outputs:
- attended: bfloat16 [24, 256, 1536], P(('clips', 'tok'), 'head'), parts along dimension 0
The draws below stay inside these ranges and needn't reach their ends.
There are 2 independent parts, one for each index of `clips`. The reference program is written for one: setup_inputs(seed, part) draws one part's arguments, and reference() takes and returns one part's arrays. A program takes and returns all parts, laid end to end along the dimension named above; each array names one. Nothing has to cross between parts.
Inputs may be any that keep to these rules, and one draw needn't show every extreme that they name: Entries of query and key lie within -16 and 16. `valid_rows`: tiles outside the last height-tile row have all 8 rows real; tiles of the last height-tile row each have their own count.
All inputs are finite; a program needn't handle non-finite values.
Results may differ from the reference program's by a relative error of at most 0.0031.
Values may be sent and summed in bfloat16 or wider, within the bound.
A program may use at most 64 MiB of HBM per device.

```python
import math
import jax
import jax.numpy as jnp
from jax import lax

HEADS = 12
HEAD_DIM = 128
TILE_H = 8
TILE_W = 8
TIME_TILES = 4
WIDTH_TILES = 3
HEIGHT_TILES = 1
TILE = 256
TILES = 12


def pair_fields(key):
    shape = (TILES, TILE, HEADS * HEAD_DIM)
    base_q = 1.6 * jnp.clip(jax.random.normal(jax.random.fold_in(key, 11), shape, jnp.float32), -4.0, 4.0)
    base_k = 1.6 * jnp.clip(jax.random.normal(jax.random.fold_in(key, 12), shape, jnp.float32), -4.0, 4.0)
    return (base_q, base_k)


def draw_query(key, part):
    return pair_fields(key)[0].astype(jnp.bfloat16)


def draw_key(key, part):
    return pair_fields(key)[1].astype(jnp.bfloat16)


def draw_valid_rows(key, part):
    tile_id = jnp.arange(TILES)
    random_counts = jax.random.randint(jax.random.fold_in(key, 21), (TILES,), 1, TILE_H + 1)
    height_pos = tile_id // WIDTH_TILES % HEIGHT_TILES
    time_pos = tile_id // (WIDTH_TILES * HEIGHT_TILES)
    bottom = height_pos == HEIGHT_TILES - 1
    bottom_counts = jnp.where(time_pos == 1, TILE_H, jnp.where(time_pos == 2, 1, random_counts))
    rows = jnp.where(bottom, bottom_counts, TILE_H)
    return rows.astype(jnp.int32)


def block_scale(rng, shape, pieces, low, high):
    gain, own = 1.0, jax.random.fold_in(rng, 6)
    for dim, blocks in pieces:
        steps = jnp.exp(jax.random.uniform(jax.random.fold_in(own, dim), (blocks,), jnp.float32, low / len(pieces), high / len(pieces)))
        gain = gain * jnp.repeat(steps, shape[dim] // blocks).reshape([-1 if axis == dim else 1 for axis in range(len(shape))])
    return gain


def scatter_about(stream_key, shape, deviation, bound, pieces=(), kind=jnp.bfloat16):
    array = jax.random.normal(stream_key, shape, jnp.float32) * deviation
    if len(pieces) > 0:
        array = block_scale(stream_key, shape, pieces, -0.22, 0.18) * array
    return jnp.clip(array, min=-bound, max=bound).astype(kind)


def setup_inputs(seed: int = 0, part: int = 0) -> dict:
    key_list = jax.random.split(jax.random.key(seed), 5)
    part_splits = jax.random.split(jax.random.fold_in(key_list[4], part), 5)
    query = draw_query(jax.random.fold_in(jax.random.fold_in(key_list[4], part), 71), part)
    key = draw_key(jax.random.fold_in(jax.random.fold_in(key_list[4], part), 71), part)
    value = scatter_about(part_splits[2], (TILES, TILE, HEADS * HEAD_DIM), 1.0, 6.0, ((0, 4), (1, 4)))
    valid_rows = draw_valid_rows(jax.random.fold_in(jax.random.fold_in(key_list[4], part), 71), part)
    return {"query": query, "key": key, "value": value, "valid_rows": valid_rows}


def reference(query, key, value, valid_rows):
    grid = (TIME_TILES, HEIGHT_TILES, WIDTH_TILES)
    scale = 1.0 / math.sqrt(HEAD_DIM)

    def per_head(field):
        return jnp.moveaxis(field.reshape(grid + (TILE, HEADS, HEAD_DIM)), 4, 0)
    counts = jnp.pad(valid_rows.reshape(grid), 1)
    count_win = jnp.stack([counts[a:a + TIME_TILES, b:b + HEIGHT_TILES, c:c + WIDTH_TILES] for a in range(3) for b in range(3) for c in range(3)], axis=-1)
    row_index = jnp.arange(TILE) // TILE_W % TILE_H
    mask = (row_index[None, None, None, None, :] < count_win[..., None]).reshape(grid + (27 * TILE,))

    def window(field):
        padded = jnp.pad(field, ((1, 1), (1, 1), (1, 1), (0, 0), (0, 0)))
        parts = [padded[a:a + TIME_TILES, b:b + HEIGHT_TILES, c:c + WIDTH_TILES] for a in range(3) for b in range(3) for c in range(3)]
        return jnp.stack(parts, axis=3).reshape(grid + (27 * TILE, HEAD_DIM))

    def one_head(items):
        q_head, k_head, v_head = items
        k_win = window(k_head)
        v_win = window(v_head)

        def one_time(inner):
            q_part, k_part, v_part, m_part = inner
            scores = jnp.einsum('bcqd,bckd->bcqk', q_part.astype(jnp.float32), k_part.astype(jnp.float32)) * scale
            scores = jnp.where(m_part[:, :, None, :], scores, -jnp.inf)
            largest = lax.optimization_barrier(jnp.max(scores, axis=-1, keepdims=True))
            weight = jnp.exp(scores - largest)
            total = lax.optimization_barrier(jnp.sum(weight, axis=-1, keepdims=True))
            rounded = weight.astype(jnp.bfloat16)
            summed = jnp.einsum('bcqk,bckd->bcqd', rounded.astype(jnp.float32), v_part.astype(jnp.float32))
            return (summed / total).astype(jnp.bfloat16)
        return lax.map(one_time, (q_head, k_win, v_win, mask))
    result = lax.map(one_head, (per_head(query), per_head(key), per_head(value)))
    result = jnp.moveaxis(result, 0, 4)
    return result.reshape(TILES, TILE, HEADS * HEAD_DIM)
```

```python
import functools
import math

import jax
import jax.numpy as jnp
from jax import lax
from jax.experimental import pallas as pl
from jax.experimental.pallas import tpu as pltpu
from jax.sharding import PartitionSpec as P

HEAD_DIM = 128
TILE_H = 8
TILE_W = 8
TIME_TILES = 4
MESH = pl.DeviceIdType.MESH
GAIN = math.log2(math.e) / math.sqrt(HEAD_DIM)


def window_slots(rows_grid):
    sides = (-1, 0, 1) if rows_grid > 1 else (0,)
    around = [(down, side) for down in (-1, 0, 1) for side in sides if (down, side) != (0, 0)]
    return [(0, 0)] + around


def kernel(
    heads_axis, rows_grid,
    q_hbm, k_hbm, v_hbm, bias_hbm, out_hbm,
    q_buf, k_buf, v_buf, bias_buf, s_buf, p_buf, inv_buf, o_buf,
    local_sem, qx_send, qx_recv, kx_send, kx_recv, vx_send, vx_recv,
    bz_send, bz_recv, kz_send, kz_recv, vz_send, vz_recv, ox_send, ox_recv,
):
    slots = window_slots(rows_grid)
    width, part = q_hbm.shape[0], q_hbm.shape[1]
    tile_len, feats = q_buf.shape[1], q_buf.shape[2]
    local = feats // HEAD_DIM
    me = lax.axis_index("head")
    tok = lax.axis_index("tok")
    time, height = tok // rows_grid, tok % rows_grid
    steps = range(1, heads_axis)
    far_first = list(reversed(steps))

    def exists(j):
        down, side = slots[j]
        ok = (time + down >= 0) & (time + down < TIME_TILES)
        if side != 0:
            ok = ok & (height + side >= 0) & (height + side < rows_grid)
        return ok

    def around(j):
        return tok + slots[j][0] * rows_grid + slots[j][1]

    def opposite(j):
        return slots.index((-slots[j][0], -slots[j][1]))

    def peer(s):
        return me ^ s

    def rows(g):
        return pl.ds(pl.multiple_of(g * part, part), part)

    def cols(g):
        return pl.ds(pl.multiple_of(g * feats, feats), feats)

    def head_cols(h):
        return pl.ds(pl.multiple_of(h * HEAD_DIM, HEAD_DIM), HEAD_DIM)

    def global_cols(g, h):
        return pl.ds(pl.multiple_of((g * local + h) * HEAD_DIM, HEAD_DIM), HEAD_DIM)

    def remote(src, dst, send, recv, device):
        return pltpu.make_async_remote_copy(
            src_ref=src, dst_ref=dst, send_sem=send, recv_sem=recv,
            device_id=device, device_id_type=MESH,
        )

    def qx(s, owner):
        return remote(q_hbm.at[:, :, cols(peer(s))], q_buf.at[:, rows(owner), :],
                      qx_send.at[s], qx_recv.at[s], {"head": peer(s)})

    def kx(s, owner):
        return remote(k_hbm.at[:, :, cols(peer(s))], k_buf.at[0, :, rows(owner), :],
                      kx_send.at[s], kx_recv.at[s], {"head": peer(s)})

    def vx(h, s, owner):
        return remote(v_hbm.at[:, :, global_cols(peer(s), h)],
                      v_buf.at[0, :, rows(owner), head_cols(h)],
                      vx_send.at[h, s], vx_recv.at[h, s], {"head": peer(s)})

    def kz(j, s, slot):
        src = k_hbm.at[:, :, cols(me)] if s == 0 else k_buf.at[0, :, rows(peer(s)), :]
        return remote(src, k_buf.at[slot, :, rows(peer(s)), :],
                      kz_send.at[j, s], kz_recv.at[slot, s], {"tok": around(j)})

    def vz(j, h, s, slot):
        src = v_hbm.at[:, :, global_cols(me, h)] if s == 0 else v_buf.at[0, :, rows(peer(s)), head_cols(h)]
        return remote(src, v_buf.at[slot, :, rows(peer(s)), head_cols(h)],
                      vz_send.at[j, h, s], vz_recv.at[slot, h, s], {"tok": around(j)})

    def bz(j, slot):
        return remote(bias_hbm, bias_buf.at[slot], bz_send.at[j], bz_recv.at[slot], {"tok": around(j)})

    def ox(h, s, owner):
        return remote(o_buf.at[:, rows(peer(s)), head_cols(h)],
                      out_hbm.at[:, :, global_cols(owner, h)],
                      ox_send.at[h, s], ox_recv.at[h, s], {"head": peer(s)})

    def each_neighbour(act):
        for j in range(1, len(slots)):
            pl.when(exists(j))(functools.partial(act, j))

    local_q = pltpu.make_async_copy(q_hbm.at[:, :, cols(me)], q_buf.at[:, rows(me), :], local_sem.at[0])
    local_k = pltpu.make_async_copy(k_hbm.at[:, :, cols(me)], k_buf.at[0, :, rows(me), :], local_sem.at[1])
    local_v = pltpu.make_async_copy(v_hbm.at[:, :, cols(me)], v_buf.at[0, :, rows(me), :], local_sem.at[2])
    local_b = pltpu.make_async_copy(bias_hbm, bias_buf.at[0], local_sem.at[3])

    barrier = pltpu.get_barrier_semaphore()
    for s in steps:
        pl.semaphore_signal(barrier, inc=1, device_id={"head": peer(s)}, device_id_type=MESH)
    partners = heads_axis - 1

    def greet(j):
        pl.semaphore_signal(barrier, inc=1, device_id={"tok": around(j)}, device_id_type=MESH)

    each_neighbour(greet)
    for j in range(1, len(slots)):
        partners = partners + jnp.where(exists(j), 1, 0)
    for copy in (local_q, local_k, local_v, local_b):
        copy.start()
    pl.semaphore_wait(barrier, partners)

    each_neighbour(lambda j: bz(j, opposite(j)).start())
    for s in far_first:
        kx(s, me).start()
    each_neighbour(lambda j: kz(j, 0, opposite(j)).start())
    for s in far_first:
        qx(s, me).start()
    for h in range(local):
        for s in far_first:
            vx(h, s, me).start()

    for j in range(1, len(slots)):
        @pl.when(jnp.logical_not(exists(j)))
        def _(j=j):
            k_buf[j] = jnp.zeros(k_buf.shape[1:], k_buf.dtype)
            v_buf[j] = jnp.zeros(v_buf.shape[1:], v_buf.dtype)
            bias_buf[j] = jnp.full(bias_buf.shape[1:], -jnp.inf, bias_buf.dtype)

    order = [1] + [s for s in far_first if s != 1] if heads_axis > 1 else []
    for s in order:
        kx(s, peer(s)).wait_recv()
        each_neighbour(lambda j, s=s: kz(j, s, opposite(j)).start())
    near = [s for s in steps if s == 1]
    later = [s for s in order if s != 1]
    for h in range(local):
        each_neighbour(lambda j, h=h: vz(j, h, 0, opposite(j)).start())
        for s in near:
            vx(h, s, peer(s)).wait_recv()
            each_neighbour(lambda j, h=h, s=s: vz(j, h, s, opposite(j)).start())

    for copy in (local_q, local_k, local_v, local_b):
        copy.wait()
    for s in steps:
        qx(s, peer(s)).wait_recv()

    def keys_in(j):
        bz(j, j).wait_recv()
        for s in range(heads_axis):
            kz(j, s, j).wait_recv()

    each_neighbour(keys_in)

    def window(c):
        return [(j, n) for j in range(len(slots)) for n in range(width) if abs(n - c) <= 1]

    def weigh(h, carry):
        for c in range(width):
            scratch = s_buf.at[c % s_buf.shape[0]]
            q = q_buf[c, :, head_cols(h)]
            top = None
            for i, (j, n) in enumerate(window(c)):
                s = lax.dot_general(q, k_buf[j, n, :, head_cols(h)], (((1,), (1,)), ((), ())),
                                    preferred_element_type=jnp.float32)
                s = s + bias_buf[j, n, 0:1, :]
                scratch[:, i * tile_len:(i + 1) * tile_len] = s
                for half in range(0, tile_len, 128):
                    piece = s[:, half:half + 128]
                    top = piece if top is None else jnp.maximum(top, piece)
            largest = jnp.max(top, axis=-1, keepdims=True)
            total = None
            for i in range(len(window(c))):
                for half in range(0, tile_len, 128):
                    at = slice(i * tile_len + half, i * tile_len + half + 128)
                    weight = jnp.exp2((scratch[:, at] - largest) * GAIN)
                    total = weight if total is None else total + weight
                    p_buf[h, c, :, at] = weight.astype(jnp.bfloat16)
            inverse = 1.0 / jnp.sum(total, axis=-1, keepdims=True)
            inv_buf[h, c] = jnp.broadcast_to(inverse, (tile_len, HEAD_DIM))
        for s in later:
            vx(h, s, peer(s)).wait_recv()
            each_neighbour(lambda j, s=s: vz(j, h, s, opposite(j)).start())
        return carry

    lax.fori_loop(0, local, weigh, 0)

    def local_out(h):
        return pltpu.make_async_copy(o_buf.at[:, rows(me), head_cols(h)],
                                     out_hbm.at[:, :, global_cols(me, h)], local_sem.at[4 + h])

    def mix(h, carry):
        def values_in(j):
            for s in range(heads_axis):
                vz(j, h, s, j).wait_recv()

        each_neighbour(values_in)
        for c in range(width):
            summed = None
            for i, (j, n) in enumerate(window(c)):
                term = jnp.dot(p_buf[h, c, :, i * tile_len:(i + 1) * tile_len],
                               v_buf[j, n, :, head_cols(h)], preferred_element_type=jnp.float32)
                summed = term if summed is None else summed + term
            o_buf[c, :, head_cols(h)] = (summed * inv_buf[h, c]).astype(o_buf.dtype)
        for s in far_first:
            ox(h, s, me).start()
        local_out(h).start()
        return carry

    lax.fori_loop(0, local, mix, 0)

    for s in steps:
        kx(s, me).wait_send()
        qx(s, me).wait_send()
        for h in range(local):
            vx(h, s, me).wait_send()

    def sent(j):
        bz(j, opposite(j)).wait_send()
        for s in range(heads_axis):
            kz(j, s, opposite(j)).wait_send()
            for h in range(local):
                vz(j, h, s, opposite(j)).wait_send()

    each_neighbour(sent)
    for h in range(local):
        local_out(h).wait()
        for s in steps:
            ox(h, s, me).wait_send()
            ox(h, s, peer(s)).wait_recv()


def body(heads_axis, tok_axis, query, key, value, valid_rows):
    width, part, wide = query.shape
    rows_grid = tok_axis // TIME_TILES
    tile_len, feats = part * heads_axis, wide // heads_axis
    local = feats // HEAD_DIM
    slots = len(window_slots(rows_grid))
    row_index = jnp.arange(tile_len) // TILE_W % TILE_H
    bias = jnp.where(row_index[None, None, :] < valid_rows[:, None, None], 0.0, -jnp.inf)
    bias = jnp.broadcast_to(bias.astype(jnp.float32), (width, 8, tile_len))
    most = slots * min(width, 3) * tile_len
    dma = pltpu.SemaphoreType.DMA
    any_space = pl.BlockSpec(memory_space=pl.ANY)
    return pl.pallas_call(
        functools.partial(kernel, heads_axis, rows_grid),
        out_shape=jax.ShapeDtypeStruct(query.shape, query.dtype),
        in_specs=[any_space] * 4,
        out_specs=any_space,
        scratch_shapes=[
            pltpu.VMEM((width, tile_len, feats), jnp.bfloat16),
            pltpu.VMEM((slots, width, tile_len, feats), jnp.bfloat16),
            pltpu.VMEM((slots, width, tile_len, feats), jnp.bfloat16),
            pltpu.VMEM((slots, width, 8, tile_len), jnp.float32),
            pltpu.VMEM((3 if slots <= 3 else 1, tile_len, most), jnp.float32),
            pltpu.VMEM((local, width, tile_len, most), jnp.bfloat16),
            pltpu.VMEM((local, width, tile_len, HEAD_DIM), jnp.float32),
            pltpu.VMEM((width, tile_len, feats), jnp.bfloat16),
            dma((4 + local,)),
            dma((heads_axis,)), dma((heads_axis,)),
            dma((heads_axis,)), dma((heads_axis,)),
            dma((local, heads_axis)), dma((local, heads_axis)),
            dma((slots,)), dma((slots,)),
            dma((slots, heads_axis)), dma((slots, heads_axis)),
            dma((slots, local, heads_axis)), dma((slots, local, heads_axis)),
            dma((local, heads_axis)), dma((local, heads_axis)),
        ],
        compiler_params=pltpu.CompilerParams(
            collective_id=0, has_side_effects=True, vmem_limit_bytes=63_000_000
        ),
    )(query, key, value, bias)


def solution(mesh):
    placed = (
        P(("clips", "tok"), "head", None),
        P(("clips", "tok"), "head", None),
        P(("clips", "tok"), "head", None),
        P(("clips", "tok")),
    )
    return jax.shard_map(
        functools.partial(body, mesh.shape["head"], mesh.shape["tok"]),
        mesh=mesh,
        in_specs=placed,
        out_specs=P(("clips", "tok"), "head", None),
        check_vma=False,
    )
```

```python
import functools
import math

import jax
import jax.numpy as jnp
from jax import lax
from jax.experimental import pallas as pl
from jax.experimental.pallas import tpu as pltpu
from jax.sharding import PartitionSpec as P

HEAD_DIM = 128
TILE_H = 8
TILE_W = 8
TIME_TILES = 4
MESH = pl.DeviceIdType.MESH
GAIN = math.log2(math.e) / math.sqrt(HEAD_DIM)


def window_slots(rows_grid):
    sides = (-1, 0, 1) if rows_grid > 1 else (0,)
    around = [(down, side) for down in (-1, 0, 1) for side in sides if (down, side) != (0, 0)]
    return [(0, 0)] + around


def kernel(
    heads_axis, rows_grid,
    q_hbm, k_hbm, v_hbm, count_hbm, out_hbm,
    q_buf, k_buf, v_buf, bias_buf, s_buf, p_buf, inv_buf, acc_buf, o_buf, count_buf,
    local_sem, qx_send, qx_recv, kx_send, kx_recv, vx_send, vx_recv,
    bz_send, bz_recv, kz_send, kz_recv, vz_send, vz_recv, ox_send, ox_recv,
):
    slots = window_slots(rows_grid)
    width, part = q_hbm.shape[0], q_hbm.shape[1]
    tile_len, feats = q_buf.shape[1], q_buf.shape[2]
    local = feats // HEAD_DIM
    me = lax.axis_index("head")
    tok = lax.axis_index("tok")
    time, height = tok // rows_grid, tok % rows_grid
    steps = range(1, heads_axis)
    far_first = list(reversed(steps))

    def exists(j):
        down, side = slots[j]
        ok = (time + down >= 0) & (time + down < TIME_TILES)
        if side != 0:
            ok = ok & (height + side >= 0) & (height + side < rows_grid)
        return ok

    def around(j):
        return tok + slots[j][0] * rows_grid + slots[j][1]

    def opposite(j):
        return slots.index((-slots[j][0], -slots[j][1]))

    def peer(s):
        return me ^ s

    def rows(g):
        return pl.ds(pl.multiple_of(g * part, part), part)

    def cols(g):
        return pl.ds(pl.multiple_of(g * feats, feats), feats)

    def head_cols(h):
        return pl.ds(pl.multiple_of(h * HEAD_DIM, HEAD_DIM), HEAD_DIM)

    def global_cols(g, h):
        return pl.ds(pl.multiple_of((g * local + h) * HEAD_DIM, HEAD_DIM), HEAD_DIM)

    def remote(src, dst, send, recv, device):
        return pltpu.make_async_remote_copy(
            src_ref=src, dst_ref=dst, send_sem=send, recv_sem=recv,
            device_id=device, device_id_type=MESH,
        )

    def qx(s, owner):
        return remote(q_hbm.at[:, :, cols(peer(s))], q_buf.at[:, rows(owner), :],
                      qx_send.at[s], qx_recv.at[s], {"head": peer(s)})

    def kx(s, owner):
        return remote(k_hbm.at[:, :, cols(peer(s))], k_buf.at[0, :, rows(owner), :],
                      kx_send.at[s], kx_recv.at[s], {"head": peer(s)})

    def vx(h, n, s, owner):
        return remote(v_hbm.at[n, :, global_cols(peer(s), h)],
                      v_buf.at[0, n, rows(owner), head_cols(h)],
                      vx_send.at[h, n, s], vx_recv.at[h, n, s], {"head": peer(s)})

    def kz(j, s, slot):
        src = k_hbm.at[:, :, cols(me)] if s == 0 else k_buf.at[0, :, rows(peer(s)), :]
        return remote(src, k_buf.at[slot, :, rows(peer(s)), :],
                      kz_send.at[j, s], kz_recv.at[slot, s], {"tok": around(j)})

    def vz(j, h, n, s, slot):
        src = v_hbm.at[n, :, global_cols(me, h)] if s == 0 else v_buf.at[0, n, rows(peer(s)), head_cols(h)]
        return remote(src, v_buf.at[slot, n, rows(peer(s)), head_cols(h)],
                      vz_send.at[j, h, n, s], vz_recv.at[slot, h, n, s], {"tok": around(j)})

    def bz(j, slot):
        return remote(bias_buf.at[0], bias_buf.at[slot], bz_send.at[j], bz_recv.at[slot], {"tok": around(j)})

    def ox(h, c, s, owner):
        return remote(o_buf.at[c, rows(peer(s)), head_cols(h)],
                      out_hbm.at[c, :, global_cols(owner, h)],
                      ox_send.at[h, c, s], ox_recv.at[h, c, s], {"head": peer(s)})

    def each_neighbour(act):
        for j in range(1, len(slots)):
            pl.when(exists(j))(functools.partial(act, j))

    local_q = pltpu.make_async_copy(q_hbm.at[:, :, cols(me)], q_buf.at[:, rows(me), :], local_sem.at[0])
    local_k = pltpu.make_async_copy(k_hbm.at[:, :, cols(me)], k_buf.at[0, :, rows(me), :], local_sem.at[1])
    local_v = pltpu.make_async_copy(v_hbm.at[:, :, cols(me)], v_buf.at[0, :, rows(me), :], local_sem.at[2])
    local_c = pltpu.make_async_copy(count_hbm, count_buf, local_sem.at[3])

    barrier = pltpu.get_barrier_semaphore()
    for s in steps:
        pl.semaphore_signal(barrier, inc=1, device_id={"head": peer(s)}, device_id_type=MESH)
    partners = heads_axis - 1

    def greet(j):
        pl.semaphore_signal(barrier, inc=1, device_id={"tok": around(j)}, device_id_type=MESH)

    each_neighbour(greet)
    for j in range(1, len(slots)):
        partners = partners + jnp.where(exists(j), 1, 0)
    for copy in (local_c, local_q, local_k, local_v):
        copy.start()
    pl.semaphore_wait(barrier, partners)

    for s in far_first:
        kx(s, me).start()
    each_neighbour(lambda j: kz(j, 0, opposite(j)).start())
    for s in far_first:
        qx(s, me).start()
    for h in range(local):
        for n in range(width):
            for s in far_first:
                vx(h, n, s, me).start()

    local_c.wait()
    row = lax.broadcasted_iota(jnp.int32, bias_buf.shape[2:], 1) // TILE_W % TILE_H
    for n in range(width):
        bias_buf[0, n] = jnp.where(row < count_buf[n], 0.0, -jnp.inf)

    for j in range(1, len(slots)):
        @pl.when(jnp.logical_not(exists(j)))
        def _(j=j):
            k_buf[j] = jnp.zeros(k_buf.shape[1:], k_buf.dtype)
            v_buf[j] = jnp.zeros(v_buf.shape[1:], v_buf.dtype)
            bias_buf[j] = jnp.full(bias_buf.shape[1:], -jnp.inf, bias_buf.dtype)

    order = [1] + [s for s in far_first if s != 1] if heads_axis > 1 else []
    for s in order:
        kx(s, peer(s)).wait_recv()
        each_neighbour(lambda j, s=s: kz(j, s, opposite(j)).start())
    near = [s for s in steps if s == 1]
    later = [s for s in order if s != 1]
    each_neighbour(lambda j: bz(j, opposite(j)).start())

    def values_on(h, n, s):
        if s != 0:
            vx(h, n, s, peer(s)).wait_recv()
        each_neighbour(lambda j: vz(j, h, n, s, opposite(j)).start())

    for h in range(local):
        for n in range(width):
            for s in [0] + near:
                values_on(h, n, s)

    for copy in (local_q, local_k, local_v):
        copy.wait()
    for s in steps:
        qx(s, peer(s)).wait_recv()

    def keys_in(j):
        bz(j, j).wait_recv()
        for s in range(heads_axis):
            kz(j, s, j).wait_recv()

    each_neighbour(keys_in)

    def window(c):
        return [(j, n) for j in range(len(slots)) for n in range(width) if abs(n - c) <= 1]

    def weigh(h, carry):
        for c in range(width):
            scratch = s_buf.at[c % s_buf.shape[0]]
            q = q_buf[c, :, head_cols(h)]
            top = None
            for i, (j, n) in enumerate(window(c)):
                s = lax.dot_general(q, k_buf[j, n, :, head_cols(h)], (((1,), (1,)), ((), ())),
                                    preferred_element_type=jnp.float32)
                s = s + bias_buf[j, n, 0:1, :]
                scratch[:, i * tile_len:(i + 1) * tile_len] = s
                for half in range(0, tile_len, 128):
                    piece = s[:, half:half + 128]
                    top = piece if top is None else jnp.maximum(top, piece)
            largest = jnp.max(top, axis=-1, keepdims=True)
            total = None
            for i in range(len(window(c))):
                for half in range(0, tile_len, 128):
                    at = slice(i * tile_len + half, i * tile_len + half + 128)
                    weight = jnp.exp2((scratch[:, at] - largest) * GAIN)
                    total = weight if total is None else total + weight
                    p_buf[h, c, :, at] = weight.astype(jnp.bfloat16)
            inverse = 1.0 / jnp.sum(total, axis=-1, keepdims=True)
            inv_buf[h, c] = jnp.broadcast_to(inverse, (tile_len, HEAD_DIM))
        for n in range(width):
            for s in later:
                values_on(h, n, s)
        return carry

    lax.fori_loop(0, local, weigh, 0)

    def local_out(h, c):
        return pltpu.make_async_copy(o_buf.at[c, rows(me), head_cols(h)],
                                     out_hbm.at[c, :, global_cols(me, h)], local_sem.at[4 + h * width + c])

    def mix(h, carry):
        def gather(c, picked):
            summed = None
            for i, (j, n) in enumerate(window(c)):
                if picked(j, n):
                    term = jnp.dot(p_buf[h, c, :, i * tile_len:(i + 1) * tile_len],
                                   v_buf[j, n, :, head_cols(h)], preferred_element_type=jnp.float32)
                    summed = term if summed is None else summed + term
            return summed

        for c in range(width):
            acc_buf[c] = gather(c, lambda j, n: j == 0)
        for n in range(width):
            def values_in(j, n=n):
                for s in range(heads_axis):
                    vz(j, h, n, s, j).wait_recv()

            each_neighbour(values_in)
            done = []
            for c in range(width):
                if abs(n - c) <= 1:
                    summed = acc_buf[c] + gather(c, lambda j, m: j != 0 and m == n)
                    if n == min(c + 1, width - 1):
                        o_buf[c, :, head_cols(h)] = (summed * inv_buf[h, c]).astype(o_buf.dtype)
                        done.append(c)
                    else:
                        acc_buf[c] = summed
            for s in far_first:
                for c in done:
                    ox(h, c, s, me).start()
            for c in done:
                local_out(h, c).start()
        return carry

    lax.fori_loop(0, local, mix, 0)

    for s in steps:
        kx(s, me).wait_send()
        qx(s, me).wait_send()
        for h in range(local):
            for n in range(width):
                vx(h, n, s, me).wait_send()

    def sent(j):
        bz(j, opposite(j)).wait_send()
        for s in range(heads_axis):
            kz(j, s, opposite(j)).wait_send()
            for h in range(local):
                for n in range(width):
                    vz(j, h, n, s, opposite(j)).wait_send()

    each_neighbour(sent)
    for h in range(local):
        for c in range(width):
            local_out(h, c).wait()
            for s in steps:
                ox(h, c, s, me).wait_send()
                ox(h, c, s, peer(s)).wait_recv()


def body(heads_axis, tok_axis, query, key, value, valid_rows):
    width, part, wide = query.shape
    rows_grid = tok_axis // TIME_TILES
    tile_len, feats = part * heads_axis, wide // heads_axis
    local = feats // HEAD_DIM
    slots = len(window_slots(rows_grid))
    most = slots * min(width, 3) * tile_len
    dma = pltpu.SemaphoreType.DMA
    any_space = pl.BlockSpec(memory_space=pl.ANY)
    return pl.pallas_call(
        functools.partial(kernel, heads_axis, rows_grid),
        out_shape=jax.ShapeDtypeStruct(query.shape, query.dtype),
        in_specs=[pl.BlockSpec(memory_space=pltpu.HBM)] * 4,
        out_specs=any_space,
        scratch_shapes=[
            pltpu.VMEM((width, tile_len, feats), jnp.bfloat16),
            pltpu.VMEM((slots, width, tile_len, feats), jnp.bfloat16),
            pltpu.VMEM((slots, width, tile_len, feats), jnp.bfloat16),
            pltpu.VMEM((slots, width, 8, tile_len), jnp.float32),
            pltpu.VMEM((3 if slots <= 3 else 1, tile_len, most), jnp.float32),
            pltpu.VMEM((local, width, tile_len, most), jnp.bfloat16),
            pltpu.VMEM((local, width, tile_len, HEAD_DIM), jnp.float32),
            pltpu.VMEM((width, tile_len, HEAD_DIM), jnp.float32),
            pltpu.VMEM((width, tile_len, feats), jnp.bfloat16),
            pltpu.SMEM((width,), jnp.int32),
            dma((4 + local * width,)),
            dma((heads_axis,)), dma((heads_axis,)),
            dma((heads_axis,)), dma((heads_axis,)),
            dma((local, width, heads_axis)), dma((local, width, heads_axis)),
            dma((slots,)), dma((slots,)),
            dma((slots, heads_axis)), dma((slots, heads_axis)),
            dma((slots, local, width, heads_axis)), dma((slots, local, width, heads_axis)),
            dma((local, width, heads_axis)), dma((local, width, heads_axis)),
        ],
        compiler_params=pltpu.CompilerParams(
            collective_id=0, has_side_effects=True, vmem_limit_bytes=36_000_000 if slots <= 3 else 63_000_000
        ),
    )(*(pltpu.with_memory_space_constraint(x, pltpu.HBM) for x in (query, key, value, valid_rows)))


def solution(mesh):
    placed = (
        P(("clips", "tok"), "head", None),
        P(("clips", "tok"), "head", None),
        P(("clips", "tok"), "head", None),
        P(("clips", "tok")),
    )
    return jax.shard_map(
        functools.partial(body, mesh.shape["head"], mesh.shape["tok"]),
        mesh=mesh,
        in_specs=placed,
        out_specs=P(("clips", "tok"), "head", None),
        check_vma=False,
    )
```

```python
import functools
import math

import jax
import jax.numpy as jnp
from jax import lax
from jax.experimental import pallas as pl
from jax.experimental.pallas import tpu as pltpu
from jax.sharding import PartitionSpec as P

HEAD_DIM = 128
TILE_H = 8
TILE_W = 8
TIME_TILES = 4
MESH = pl.DeviceIdType.MESH
GAIN = math.log2(math.e) / math.sqrt(HEAD_DIM)


def window_slots(rows_grid):
    sides = (-1, 0, 1) if rows_grid > 1 else (0,)
    around = [(down, side) for down in (-1, 0, 1) for side in sides if (down, side) != (0, 0)]
    return [(0, 0)] + around


def kernel(
    heads_axis, rows_grid,
    q_hbm, k_hbm, v_hbm, count_hbm, out_hbm,
    q_buf, k_buf, v_buf, bias_buf, s_buf, p_buf, inv_buf, acc_buf, o_buf, rows_buf, count_buf,
    local_sem, qx_send, qx_recv, kx_send, kx_recv, vx_send, vx_recv,
    bz_send, bz_recv, kz_send, kz_recv, vz_send, vz_recv, ox_send, ox_recv,
):
    slots = window_slots(rows_grid)
    width, part = q_hbm.shape[0], q_hbm.shape[1]
    tile_len, feats = q_buf.shape[1], q_buf.shape[2]
    local = feats // HEAD_DIM
    me = lax.axis_index("head")
    tok = lax.axis_index("tok")
    time, height = tok // rows_grid, tok % rows_grid
    steps = range(1, heads_axis)
    far_first = list(reversed(steps))

    def exists(j):
        down, side = slots[j]
        ok = (time + down >= 0) & (time + down < TIME_TILES)
        if side != 0:
            ok = ok & (height + side >= 0) & (height + side < rows_grid)
        return ok

    def around(j):
        return tok + slots[j][0] * rows_grid + slots[j][1]

    def opposite(j):
        return slots.index((-slots[j][0], -slots[j][1]))

    def peer(s):
        return me ^ s

    def rows(g):
        return pl.ds(pl.multiple_of(g * part, part), part)

    def cols(g):
        return pl.ds(pl.multiple_of(g * feats, feats), feats)

    def head_cols(h):
        return pl.ds(pl.multiple_of(h * HEAD_DIM, HEAD_DIM), HEAD_DIM)

    def global_cols(g, h):
        return pl.ds(pl.multiple_of((g * local + h) * HEAD_DIM, HEAD_DIM), HEAD_DIM)

    def remote(src, dst, send, recv, device):
        return pltpu.make_async_remote_copy(
            src_ref=src, dst_ref=dst, send_sem=send, recv_sem=recv,
            device_id=device, device_id_type=MESH,
        )

    def qx(s, owner):
        return remote(q_hbm.at[:, :, cols(peer(s))], q_buf.at[:, rows(owner), :],
                      qx_send.at[s], qx_recv.at[s], {"head": peer(s)})

    def kx(s, owner):
        return remote(k_hbm.at[:, :, cols(peer(s))], k_buf.at[0, :, rows(owner), :],
                      kx_send.at[s], kx_recv.at[s], {"head": peer(s)})

    def vx(h, n, s, owner):
        return remote(v_hbm.at[n, :, global_cols(peer(s), h)],
                      v_buf.at[0, n, rows(owner), head_cols(h)],
                      vx_send.at[h, n, s], vx_recv.at[h, n, s], {"head": peer(s)})

    def kz(j, s, slot):
        src = k_hbm.at[:, :, cols(me)] if s == 0 else k_buf.at[0, :, rows(peer(s)), :]
        return remote(src, k_buf.at[slot, :, rows(peer(s)), :],
                      kz_send.at[j, s], kz_recv.at[slot, s], {"tok": around(j)})

    def vz(j, h, n, s, slot):
        src = v_hbm.at[n, :, global_cols(me, h)] if s == 0 else v_buf.at[0, n, rows(peer(s)), head_cols(h)]
        return remote(src, v_buf.at[slot, n, rows(peer(s)), head_cols(h)],
                      vz_send.at[j, h, n, s], vz_recv.at[slot, h, n, s], {"tok": around(j)})

    def bz(j, slot):
        return remote(rows_buf.at[0], rows_buf.at[slot], bz_send.at[j], bz_recv.at[slot], {"tok": around(j)})

    def ox(h, c, s, owner):
        return remote(o_buf.at[c, rows(peer(s)), head_cols(h)],
                      out_hbm.at[c, :, global_cols(owner, h)],
                      ox_send.at[h, c, s], ox_recv.at[h, c, s], {"head": peer(s)})

    def each_neighbour(act):
        for j in range(1, len(slots)):
            pl.when(exists(j))(functools.partial(act, j))

    local_q = pltpu.make_async_copy(q_hbm.at[:, :, cols(me)], q_buf.at[:, rows(me), :], local_sem.at[0])
    local_k = pltpu.make_async_copy(k_hbm.at[:, :, cols(me)], k_buf.at[0, :, rows(me), :], local_sem.at[1])
    local_v = pltpu.make_async_copy(v_hbm.at[:, :, cols(me)], v_buf.at[0, :, rows(me), :], local_sem.at[2])
    local_c = pltpu.make_async_copy(count_hbm, count_buf, local_sem.at[3])

    barrier = pltpu.get_barrier_semaphore()
    for s in steps:
        pl.semaphore_signal(barrier, inc=1, device_id={"head": peer(s)}, device_id_type=MESH)
    partners = heads_axis - 1

    def greet(j):
        pl.semaphore_signal(barrier, inc=1, device_id={"tok": around(j)}, device_id_type=MESH)

    each_neighbour(greet)
    for j in range(1, len(slots)):
        partners = partners + jnp.where(exists(j), 1, 0)
    for copy in (local_c, local_q, local_k, local_v):
        copy.start()
    pl.semaphore_wait(barrier, partners)

    for s in far_first:
        kx(s, me).start()
    each_neighbour(lambda j: kz(j, 0, opposite(j)).start())
    for s in far_first:
        qx(s, me).start()
    for h in range(local):
        for n in range(width):
            for s in far_first:
                vx(h, n, s, me).start()

    local_c.wait()
    line = lax.broadcasted_iota(jnp.int32, rows_buf.shape[1:], 0)
    counts = jnp.zeros(rows_buf.shape[1:], jnp.int32)
    for n in range(width):
        counts = jnp.where(line == n, count_buf[n], counts)
    rows_buf[0] = counts

    for j in range(1, len(slots)):
        @pl.when(jnp.logical_not(exists(j)))
        def _(j=j):
            k_buf[j] = jnp.zeros(k_buf.shape[1:], k_buf.dtype)
            v_buf[j] = jnp.zeros(v_buf.shape[1:], v_buf.dtype)
            rows_buf[j] = jnp.zeros(rows_buf.shape[1:], rows_buf.dtype)

    order = [1] + [s for s in far_first if s != 1] if heads_axis > 1 else []
    for s in order:
        kx(s, peer(s)).wait_recv()
        each_neighbour(lambda j, s=s: kz(j, s, opposite(j)).start())
    near = [s for s in steps if s == 1]
    later = [s for s in order if s != 1]
    each_neighbour(lambda j: bz(j, opposite(j)).start())

    def values_on(h, n, s):
        if s != 0:
            vx(h, n, s, peer(s)).wait_recv()
        each_neighbour(lambda j: vz(j, h, n, s, opposite(j)).start())

    for h in range(local):
        for n in range(width):
            for s in [0] + near:
                values_on(h, n, s)

    for copy in (local_q, local_k, local_v):
        copy.wait()
    for s in steps:
        qx(s, peer(s)).wait_recv()

    def keys_in(j):
        bz(j, j).wait_recv()
        for s in range(heads_axis):
            kz(j, s, j).wait_recv()

    each_neighbour(keys_in)

    row = lax.broadcasted_iota(jnp.int32, bias_buf.shape[2:], 1) // TILE_W % TILE_H
    for j in range(len(slots)):
        for n in range(width):
            real = jnp.broadcast_to(rows_buf[j, n:n + 1, 0:1], row.shape)
            bias_buf[j, n] = jnp.where(row < real, 0.0, -jnp.inf)

    def window(c):
        return [(j, n) for j in range(len(slots)) for n in range(width) if abs(n - c) <= 1]

    def weigh(h, carry):
        for c in range(width):
            scratch = s_buf.at[c % s_buf.shape[0]]
            q = q_buf[c, :, head_cols(h)]
            top = None
            for i, (j, n) in enumerate(window(c)):
                s = lax.dot_general(q, k_buf[j, n, :, head_cols(h)], (((1,), (1,)), ((), ())),
                                    preferred_element_type=jnp.float32)
                s = s + bias_buf[j, n, 0:1, :]
                scratch[:, i * tile_len:(i + 1) * tile_len] = s
                for half in range(0, tile_len, 128):
                    piece = s[:, half:half + 128]
                    top = piece if top is None else jnp.maximum(top, piece)
            largest = jnp.max(top, axis=-1, keepdims=True)
            total = None
            for i in range(len(window(c))):
                for half in range(0, tile_len, 128):
                    at = slice(i * tile_len + half, i * tile_len + half + 128)
                    weight = jnp.exp2((scratch[:, at] - largest) * GAIN)
                    total = weight if total is None else total + weight
                    p_buf[h, c, :, at] = weight.astype(jnp.bfloat16)
            inverse = 1.0 / jnp.sum(total, axis=-1, keepdims=True)
            inv_buf[h, c] = jnp.broadcast_to(inverse, (tile_len, HEAD_DIM))
        for n in range(width):
            for s in later:
                values_on(h, n, s)
        return carry

    lax.fori_loop(0, local, weigh, 0)

    def local_out(h, c):
        return pltpu.make_async_copy(o_buf.at[c, rows(me), head_cols(h)],
                                     out_hbm.at[c, :, global_cols(me, h)], local_sem.at[4 + h * width + c])

    if heads_axis % 2 == 0:
        half = heads_axis // 2
        span = tile_len // 2
        side = me // half
        blocks = [
            (pl.ds(pl.multiple_of((1 - side) * span, span), span), [s for s in far_first if s >= half]),
            (pl.ds(pl.multiple_of(side * span, span), span), [s for s in far_first if s < half]),
        ]
    else:
        blocks = [(slice(None), far_first)]

    def mix(h, carry):
        def gather(c, at, picked):
            summed = None
            for i, (j, n) in enumerate(window(c)):
                if picked(j, n):
                    term = jnp.dot(p_buf[h, c, at, i * tile_len:(i + 1) * tile_len],
                                   v_buf[j, n, :, head_cols(h)], preferred_element_type=jnp.float32)
                    summed = term if summed is None else summed + term
            return summed

        for c in range(width):
            acc_buf[c] = gather(c, slice(None), lambda j, n: j == 0)
        for n in range(width):
            def values_in(j, n=n):
                for s in range(heads_axis):
                    vz(j, h, n, s, j).wait_recv()

            each_neighbour(values_in)
            here = [c for c in range(width) if abs(n - c) <= 1]
            done = [c for c in here if n == min(c + 1, width - 1)]
            for at, partners_at in blocks:
                for c in done:
                    summed = acc_buf[c, at] + gather(c, at, lambda j, m: j != 0 and m == n)
                    o_buf[c, at, head_cols(h)] = (summed * inv_buf[h, c, at]).astype(o_buf.dtype)
                    for s in partners_at:
                        ox(h, c, s, me).start()
            for c in done:
                local_out(h, c).start()
            for c in here:
                if c not in done:
                    acc_buf[c] = acc_buf[c] + gather(c, slice(None), lambda j, m: j != 0 and m == n)
        return carry

    lax.fori_loop(0, local, mix, 0)

    for s in steps:
        kx(s, me).wait_send()
        qx(s, me).wait_send()
        for h in range(local):
            for n in range(width):
                vx(h, n, s, me).wait_send()

    def sent(j):
        bz(j, opposite(j)).wait_send()
        for s in range(heads_axis):
            kz(j, s, opposite(j)).wait_send()
            for h in range(local):
                for n in range(width):
                    vz(j, h, n, s, opposite(j)).wait_send()

    each_neighbour(sent)
    for h in range(local):
        for c in range(width):
            local_out(h, c).wait()
            for s in steps:
                ox(h, c, s, me).wait_send()
                ox(h, c, s, peer(s)).wait_recv()


def body(heads_axis, tok_axis, query, key, value, valid_rows):
    width, part, wide = query.shape
    rows_grid = tok_axis // TIME_TILES
    tile_len, feats = part * heads_axis, wide // heads_axis
    local = feats // HEAD_DIM
    slots = len(window_slots(rows_grid))
    most = slots * min(width, 3) * tile_len
    dma = pltpu.SemaphoreType.DMA
    any_space = pl.BlockSpec(memory_space=pl.ANY)
    return pl.pallas_call(
        functools.partial(kernel, heads_axis, rows_grid),
        out_shape=jax.ShapeDtypeStruct(query.shape, query.dtype),
        in_specs=[pl.BlockSpec(memory_space=pltpu.HBM)] * 4,
        out_specs=any_space,
        scratch_shapes=[
            pltpu.VMEM((width, tile_len, feats), jnp.bfloat16),
            pltpu.VMEM((slots, width, tile_len, feats), jnp.bfloat16),
            pltpu.VMEM((slots, width, tile_len, feats), jnp.bfloat16),
            pltpu.VMEM((slots, width, 8, tile_len), jnp.float32),
            pltpu.VMEM((3 if slots <= 3 else 1, tile_len, most), jnp.float32),
            pltpu.VMEM((local, width, tile_len, most), jnp.bfloat16),
            pltpu.VMEM((local, width, tile_len, HEAD_DIM), jnp.float32),
            pltpu.VMEM((width, tile_len, HEAD_DIM), jnp.float32),
            pltpu.VMEM((width, tile_len, feats), jnp.bfloat16),
            pltpu.VMEM((slots, -(-width // 8) * 8, 128), jnp.int32),
            pltpu.SMEM((width,), jnp.int32),
            dma((4 + local * width,)),
            dma((heads_axis,)), dma((heads_axis,)),
            dma((heads_axis,)), dma((heads_axis,)),
            dma((local, width, heads_axis)), dma((local, width, heads_axis)),
            dma((slots,)), dma((slots,)),
            dma((slots, heads_axis)), dma((slots, heads_axis)),
            dma((slots, local, width, heads_axis)), dma((slots, local, width, heads_axis)),
            dma((local, width, heads_axis)), dma((local, width, heads_axis)),
        ],
        compiler_params=pltpu.CompilerParams(
            collective_id=0, has_side_effects=True, vmem_limit_bytes=36_000_000 if slots <= 3 else 63_000_000
        ),
    )(*(pltpu.with_memory_space_constraint(x, pltpu.HBM) for x in (query, key, value, valid_rows)))


def solution(mesh):
    placed = (
        P(("clips", "tok"), "head", None),
        P(("clips", "tok"), "head", None),
        P(("clips", "tok"), "head", None),
        P(("clips", "tok")),
    )
    return jax.shard_map(
        functools.partial(body, mesh.shape["head"], mesh.shape["tok"]),
        mesh=mesh,
        in_specs=placed,
        out_specs=P(("clips", "tok"), "head", None),
        check_vma=False,
    )
```
